256 devices in a mesh: section: 8 (over x, core), expert: 32 (over y, z).
Axes of the slice: x: 4, y: 4, z: 8, core: 2. Of those that a mesh axis runs over, the one named last changes fastest.
Arguments:
- tokens: bfloat16 [2, 512, 2048], P(None, 'expert'), may hold values from -6 to 6
- norm_gain: float32 [8, 2048], P('section'), may hold values from 0.1 to 1.9
- w_gate: bfloat16 [8, 2048, 24576], P('section', None, 'expert'), may hold values from -0.125 to 0.125
- w_up: bfloat16 [8, 2048, 24576], P('section', None, 'expert'), may hold values from -0.125 to 0.125
- w_down: bfloat16 [8, 24576, 2048], P('section', 'expert'), may hold values from -0.15625 to 0.15625
- routes: int32 [8, 2, 512, 2], P('section', None, 'expert'), may hold values from 0 to 15, all different within a row; in each aligned block of 16 rows (0 to 15, 16 to 31, ..., all dimensions but the last counted through in order) at most 4 rows name the same one
- route_weights: float32 [8, 2, 512, 2], P('section', None, 'expert'), may hold values from 0.25 to 1
Outputs:
- hidden: bfloat16 [8, 2, 512, 2048], P('section', None, 'expert')
The draws below stay inside these ranges and needn't reach their ends.
Inputs may be any that keep to these rules, and one draw needn't show every extreme that they name: `routes`: each token names 2 different experts. Within the tokens of one device (aligned blocks of 16 rows, for every layer and micro-batch), no expert is named by more than 4 of the token choices, and in some blocks one expert by exactly 4.
All inputs are finite; a program needn't handle non-finite values.
Results may differ from the reference program's by a relative error of at most 0.025.
Values may be sent and summed in bfloat16 or wider, within the bound.
A program may use at most 64 MiB of HBM per device.

```python
import math
import jax
import jax.numpy as jnp
import numpy as np
from jax import lax

D = 2048
FF = 1536
FF_DEV = 768
TOP = 2
MB = 2
TOK_DEV = 16
LAYERS = 8
EXPERTS = 16
TOKENS = 512
CAP = 4
N_EXPERT = 32


def level_of(stream_key, dims, pieces, least, top_value):
    def one(position, shards_of):
        draws = jax.random.uniform(jax.random.fold_in(jax.random.fold_in(stream_key, 6), position), (shards_of,), jnp.float32, least / len(pieces), top_value / len(pieces))
        return jnp.repeat(jnp.exp(draws), dims[position] // shards_of).reshape((-1,) + (1,) * (len(dims) - position - 1))

    factor_of = one(*pieces[0])
    for cut in pieces[1:]:
        factor_of = factor_of * one(*cut)
    return factor_of


def deal_out(stream_key, own, number, rows, amount, top, limit, slope):
    order = jax.random.permutation(stream_key, amount)
    heavy_load, common = load_shares(amount, rows * top, limit, slope, True), load_shares(amount, rows * top, limit, slope, False)
    places = jnp.arange(amount)

    def named(tallies, offset_by):
        used = int((tallies > 0).sum())
        fixed = max(1, used // 4)
        passed = fixed + (places - fixed + offset_by * (used - fixed)) % max(1, amount - fixed)
        return jnp.zeros((amount,), jnp.int32).at[order[jnp.where(places < fixed, places, passed)]].set(jnp.asarray(tallies, jnp.int32))

    tallies = jnp.where(number % 4 == 0, named(heavy_load, number // 4), named(common, number - number // 4 - 1))
    mixed = jax.random.permutation(jax.random.fold_in(own, 3), amount)
    source_of, taker = mixed[0:amount // 2 * 2:2], mixed[1:amount // 2 * 2:2]
    margin = jnp.minimum(tallies[source_of] - 1, limit - tallies[taker]) // 2
    margin = jnp.where((source_of == order[0]) | (taker == order[0]) | (tallies[taker] == 0), 0, jnp.maximum(margin, 0))
    passed = jax.random.randint(jax.random.fold_in(own, 4), (amount // 2,), 0, 1 << 20) % (margin + 1)
    tallies = tallies.at[source_of].add(-passed).at[taker].add(passed)
    items = jnp.searchsorted(jnp.cumsum(tallies), jnp.arange(rows * top), side="right").astype(jnp.int32)
    table = items.reshape(top, rows).T
    table = table[jax.random.permutation(jax.random.fold_in(own, 1), rows)]
    offset_by = jax.random.randint(jax.random.fold_in(own, 2), (rows, 1), 0, top)
    return jnp.take_along_axis(table, (jnp.arange(top)[None, :] + offset_by) % top, axis=1)


def load_shares(number_of, total, bound, lean, full):
    loads = [(1 << 20) // math.isqrt(standing ** lean) + 1 for standing in range(1, number_of + 1)]
    largest = bound if full else min(bound, max(-(-total // number_of), total * loads[0] // sum(loads)))
    least = 1 if total - largest >= number_of - 1 else 0
    given, spare = [largest] + [least] * (number_of - 1), total - largest - least * (number_of - 1)
    while spare > 0:
        free = [i for i in range(1, number_of) if given[i] < largest] or [i for i in range(1, number_of) if given[i] < bound]
        pool, left = sum([loads[i] for i in free]), spare
        for i in free:
            addition = min(bound - given[i], max(1, left * loads[i] // pool), spare)
            given[i] = given[i] + addition
            spare = spare - addition
    return np.array(given)


def gaussian(own_key, shape, scale, reach, pieces=(), held_as=jnp.bfloat16):
    drawn = scale * jax.random.normal(own_key, shape, jnp.float32)
    if pieces:
        drawn = drawn * level_of(own_key, shape, pieces, -0.22, 0.18)
    return jnp.clip(drawn, -reach, reach).astype(held_as)


def setup_inputs(seed: int = 0) -> dict:
    streams_of = jax.random.split(jax.random.key(seed), 8)
    tokens = gaussian(streams_of[0], (MB, TOKENS, D), 1.0, 6.0, ((1, 32),))
    norm_gain = jnp.clip(1.0 + 0.18 * jax.random.normal(streams_of[1], (LAYERS, D), jnp.float32), 0.1, 1.9)
    w_gate = gaussian(streams_of[2], (LAYERS, D, EXPERTS * FF), D ** -0.5, 0.125, ((0, 8), (2, 32)))
    w_up = gaussian(streams_of[3], (LAYERS, D, EXPERTS * FF), D ** -0.5, 0.125, ((0, 8), (2, 32)))
    w_down = gaussian(streams_of[4], (LAYERS, EXPERTS * FF, D), FF ** -0.5, 0.15625, ((0, 8), (1, 32)))
    routes_keys = jax.random.split(jax.random.fold_in(streams_of[5], 1), LAYERS * MB * TOKENS // TOK_DEV)
    routes_turns = jax.random.permutation(jax.random.fold_in(streams_of[5], 3), LAYERS * MB * TOKENS // TOK_DEV)
    routes = jax.vmap(lambda own, number: deal_out(jax.random.fold_in(streams_of[5], 2), own, number, TOK_DEV, EXPERTS, TOP, CAP, 2))(routes_keys, routes_turns).reshape((LAYERS, MB, TOKENS, TOP))
    route_weights = jnp.clip(0.25 + 0.75 * jax.random.uniform(streams_of[6], (LAYERS, MB, TOKENS, TOP), jnp.float32) ** level_of(streams_of[6], (LAYERS, MB, TOKENS, TOP), ((0, 8), (2, 32)), -0.2, 0.2), 0.25, 1.0)
    return dict(tokens=tokens, norm_gain=norm_gain, w_gate=w_gate, w_up=w_up, w_down=w_down, routes=routes, route_weights=route_weights)


def normalize(layer_in, gain_row):
    wide_input = layer_in.astype(jnp.float32)
    inv_rms = lax.rsqrt(lax.optimization_barrier(jnp.mean(wide_input * wide_input, axis=-1, keepdims=True)) + 1e-06)
    return (wide_input, (wide_input * inv_rms * gain_row).astype(jnp.bfloat16))

def expert_half(flat_rows, gate_cols, up_cols, down_rows):
    gate_act = jnp.dot(flat_rows, gate_cols, preferred_element_type=jnp.float32)
    up_act = jnp.dot(flat_rows, up_cols, preferred_element_type=jnp.float32)
    product = (jax.nn.silu(gate_act) * up_act).astype(jnp.bfloat16)
    return jnp.dot(product, down_rows, preferred_element_type=jnp.float32).astype(jnp.bfloat16)

def moe_layer(layer_in, gain_row, picked, weights, w_gate, w_up, w_down):
    wide_input, normed = normalize(layer_in, gain_row)
    choices = picked.reshape(-1).astype(jnp.int32)
    onehot = (choices[:, None] == jnp.arange(EXPERTS, dtype=jnp.int32)[None, :]).astype(jnp.int32)
    earlier = jnp.cumsum(onehot, axis=0) - onehot
    slot_idx = lax.optimization_barrier(jnp.sum(earlier * onehot, axis=1)).astype(jnp.int32)
    owners = jnp.repeat(jnp.arange(TOKENS, dtype=jnp.int32), TOP)
    room_rows = N_EXPERT * CAP
    buffer = jnp.zeros((EXPERTS, room_rows, D), normed.dtype).at[choices, slot_idx].set(normed[owners])

    def expert_fn(expert_item):
        flat_rows, expert_idx = expert_item
        col_start = expert_idx * FF
        gate_cols = lax.dynamic_slice_in_dim(w_gate, col_start, FF, 1)
        up_cols = lax.dynamic_slice_in_dim(w_up, col_start, FF, 1)
        down_rows = lax.dynamic_slice_in_dim(w_down, col_start, FF, 0)
        first_part = expert_half(flat_rows, gate_cols[:, :FF_DEV], up_cols[:, :FF_DEV], down_rows[:FF_DEV])
        second_part = expert_half(flat_rows, gate_cols[:, FF_DEV:], up_cols[:, FF_DEV:], down_rows[FF_DEV:])
        return (first_part.astype(jnp.float32) + second_part.astype(jnp.float32)).astype(jnp.bfloat16)
    results = lax.map(expert_fn, (buffer, jnp.arange(EXPERTS, dtype=jnp.int32)))
    gathered = results[choices, slot_idx].astype(jnp.float32)
    weighted = weights.reshape(-1)[:, None].astype(jnp.float32) * gathered
    mixing = lax.optimization_barrier(jnp.sum(weighted.reshape(TOKENS, TOP, D), axis=1))
    return (wide_input + mixing).astype(jnp.bfloat16)

def reference(tokens, norm_gain, w_gate, w_up, w_down, routes, route_weights):
    carried = [tokens[micro_pos] for micro_pos in range(MB)]
    collected = []
    for layer_idx in range(LAYERS):
        layer_rows = []
        for micro_pos in range(MB):
            carried[micro_pos] = moe_layer(carried[micro_pos], norm_gain[layer_idx], routes[layer_idx, micro_pos], route_weights[layer_idx, micro_pos], w_gate[layer_idx], w_up[layer_idx], w_down[layer_idx])
            layer_rows.append(carried[micro_pos])
        collected.append(jnp.stack(layer_rows))
    return jnp.stack(collected)
```

```python
import functools

import jax
import jax.numpy as jnp
from jax import lax
from jax.experimental import pallas as pl
from jax.experimental.pallas import tpu as pltpu
from jax.sharding import PartitionSpec as P

MESH = pl.DeviceIdType.MESH
CAP = 4
PIECES = 4
UNIT = CAP * PIECES
GROUP = 16
Z_SIZE = 8

F32 = jnp.float32
BF16 = jnp.bfloat16
I32 = jnp.int32


def iota(shape, dim):
    return lax.broadcasted_iota(I32, shape, dim)


def matmul(a, b):
    return jnp.dot(a, b, preferred_element_type=F32)


def matmul_nt(a, b):
    return lax.dot_general(a, b, (((1,), (1,)), ((), ())), preferred_element_type=F32)


def far_first(step, size):
    half = (step + 1) // 2
    return size // 2 + half * (1 - 2 * (step % 2))


def kernel(
    sections,
    devices,
    z_size,
    tokens_ref,
    gain_ref,
    gate_hbm,
    up_hbm,
    down_hbm,
    routes_ref,
    weights_ref,
    out_ref,
    gate_vm,
    up_vm,
    down_vm,
    x_vm,
    prev_vm,
    hid_vm,
    pack_vm,
    zmat_vm,
    mix_vm,
    mix_in,
    perm_vm,
    permt_vm,
    dsend,
    drecv,
    rsend,
    rrecv,
    arranged,
    act_vm,
    part_vm,
    w_sem,
    ds_sem,
    dr_sem,
    rs_sem,
    rr_sem,
    xs_sem,
    xr_sem,
    hs_sem,
    hr_sem,
    ms_sem,
    mr_sem,
):
    sec = lax.axis_index("section")
    me = lax.axis_index("expert")
    micro, tok, width = x_vm.shape
    part_w = width // PIECES
    experts = devices // 2
    slots = experts * CAP
    y_size = devices // z_size
    groups = devices // GROUP
    last = sections - 1
    first_sec = sec == 0
    last_sec = sec == last
    nxt = jnp.minimum(sec + 1, last)
    prv = jnp.maximum(sec - 1, 0)
    ret_base = micro * jnp.where(last_sec, 1, 0)

    weight_copies = [
        pltpu.make_async_copy(gate_hbm.at[0], gate_vm, w_sem.at[0]),
        pltpu.make_async_copy(up_hbm.at[0], up_vm, w_sem.at[1]),
        pltpu.make_async_copy(down_hbm.at[0], down_vm, w_sem.at[2]),
    ]
    for copy in weight_copies:
        copy.start()

    barrier = pltpu.get_barrier_semaphore()

    def greet_section(i, carry):
        pl.semaphore_signal(
            barrier, inc=1, device_id=(sec, lax.rem(me + i, devices)), device_id_type=MESH
        )
        return carry

    def greet_prev(i, carry):
        pl.semaphore_signal(
            barrier, inc=1, device_id=(prv, lax.rem(me + i, devices)), device_id_type=MESH
        )
        return carry

    lax.fori_loop(1, devices, greet_section, 0)

    @pl.when(jnp.logical_not(first_sec))
    def _():
        lax.fori_loop(0, devices, greet_prev, 0)

    @pl.when(jnp.logical_not(last_sec))
    def _():
        pl.semaphore_signal(barrier, inc=1, device_id=(nxt, me), device_id_type=MESH)

    def tables(m, carry):
        picked = routes_ref[0, m]
        share = weights_ref[0, m]
        choice = jnp.concatenate([picked[:, 0:1], picked[:, 1:2]], axis=0)
        scale = jnp.concatenate([share[:, 0:1], share[:, 1:2]], axis=0)
        count = 2 * tok
        onehot = (choice == iota((count, experts), 1)).astype(F32)
        below = (iota((count, count), 1) < iota((count, count), 0)).astype(BF16)
        earlier = matmul(below, onehot.astype(BF16))
        slot = jnp.sum(earlier * onehot, axis=1, keepdims=True).astype(I32)
        place = choice * CAP + slot
        hit = (place == iota((count, slots), 1)).astype(F32)
        index_row = iota((8, slots), 1).astype(BF16)
        row0 = matmul_nt(index_row, jnp.concatenate([hit[:tok]] * PIECES, axis=0).astype(BF16))
        row1 = matmul_nt(index_row, jnp.concatenate([hit[tok:]] * PIECES, axis=0).astype(BF16))
        shape = (experts * UNIT, PIECES * tok)
        r, c = iota(shape, 0), iota(shape, 1)
        want = (r // UNIT) * CAP + r % CAP
        same = (r // CAP) % PIECES == c // tok
        names = (row0[0:1].astype(I32) == want) | (row1[0:1].astype(I32) == want)
        pack_vm[m] = (names & same).astype(F32).astype(BF16)
        lane = iota((count, devices * CAP), 1)
        lands = (lane // (2 * CAP)) * CAP + lane % CAP == place
        weighted = jnp.where(lands, scale, 0.0)
        mix_vm[m] = weighted[:tok] + weighted[tok:]
        return carry

    def spread(mix, m):
        high = mix.astype(BF16)
        rest = mix - high.astype(F32)
        mid = rest.astype(BF16)
        low = (rest - mid.astype(F32)).astype(BF16)
        terms = jnp.concatenate([high, mid, low], axis=0)
        shape = (devices * CAP, devices * UNIT)
        j, c = iota(shape, 0), iota(shape, 1)
        widen = ((c // UNIT == j // CAP) & (c % CAP == j % CAP)).astype(F32).astype(BF16)
        wide = matmul(terms, widen)
        lane = iota((tok, devices * UNIT), 1)
        rows = []
        for term in range(3):
            block = wide[term * tok : (term + 1) * tok]
            for piece in range(PIECES):
                rows.append(jnp.where((lane // CAP) % PIECES == piece, block, 0.0))
        zmat_vm[m] = jnp.concatenate(rows, axis=0).astype(BF16)

    def permutations():
        size = GROUP * UNIT
        r, c = iota((size, size), 0), iota((size, size), 1)

        def moved(a, b):
            return (
                (a // (GROUP * CAP) == (b // CAP) % PIECES)
                & ((a // CAP) % GROUP == b // UNIT)
                & (a % CAP == b % CAP)
            )

        perm_vm[...] = moved(r, c).astype(F32).astype(BF16)
        permt_vm[...] = moved(c, r).astype(F32).astype(BF16)

    lax.fori_loop(0, micro, tables, 0)

    mix_copy = pltpu.make_async_remote_copy(
        src_ref=mix_vm,
        dst_ref=mix_in,
        send_sem=ms_sem,
        recv_sem=mr_sem,
        device_id=(nxt, me),
        device_id_type=MESH,
    )

    def pieces_of(value):
        return [value[:, k * part_w : (k + 1) * part_w] for k in range(PIECES)]

    def combine(m, base, x_pieces):
        total = matmul(zmat_vm[m], rrecv[base])
        rows = PIECES * tok
        summed = (total[2 * rows :] + total[rows : 2 * rows]) + total[:rows]
        return [
            (x_pieces[k].astype(F32) + summed[k * tok : (k + 1) * tok]).astype(BF16)
            for k in range(PIECES)
        ]

    def x_copy(m):
        return pltpu.make_async_remote_copy(
            src_ref=x_vm.at[m],
            dst_ref=prev_vm.at[m],
            send_sem=xs_sem.at[m],
            recv_sem=xr_sem.at[m],
            device_id=(nxt, me),
            device_id_type=MESH,
        )

    def hid_copy(m):
        return pltpu.make_async_remote_copy(
            src_ref=x_vm.at[m],
            dst_ref=hid_vm.at[m],
            send_sem=hs_sem.at[m],
            recv_sem=hr_sem.at[m],
            device_id=(prv, me),
            device_id_type=MESH,
        )

    def wait_block(buffer, sem):
        pltpu.make_async_copy(buffer, buffer, sem).wait()

    def target(i):
        y = lax.rem(me // z_size + far_first(i % y_size, y_size), y_size)
        z = lax.rem(me % z_size + far_first(i // y_size, z_size), z_size)
        return y * z_size + z

    def micro_batch(m, carry):
        @pl.when(first_sec)
        def _():
            x_vm[m] = tokens_ref[m]

        @pl.when(jnp.logical_not(first_sec))
        def _():
            @pl.when(m == 0)
            def _():
                wait_block(mix_in, mr_sem)

                def widen(k, carry):
                    spread(mix_in[k], k)
                    return carry

                lax.fori_loop(0, micro, widen, 0)

            wait_block(prev_vm.at[m], xr_sem.at[m])
            wait_block(rrecv.at[m], rr_sem.at[m])
            done = combine(m, m, pieces_of(prev_vm[m]))
            for k in range(PIECES):
                x_vm[m, :, k * part_w : (k + 1) * part_w] = done[k]

        wide = x_vm[m].astype(F32)
        mean = jnp.mean(wide * wide, axis=-1, keepdims=True)
        normed = (wide * lax.rsqrt(mean + 1e-06) * gain_ref[...]).astype(BF16)
        stacked = jnp.concatenate(pieces_of(normed), axis=0)
        dsend[m] = matmul(pack_vm[m], stacked).astype(BF16)

        def send_rows(i, carry):
            to = target(i)
            pltpu.make_async_remote_copy(
                src_ref=dsend.at[m, pl.ds(pl.multiple_of((to // 2) * UNIT, UNIT), UNIT)],
                dst_ref=drecv.at[m, pl.ds(pl.multiple_of(me * UNIT, UNIT), UNIT)],
                send_sem=ds_sem.at[m],
                recv_sem=dr_sem.at[m],
                device_id=(sec, to),
                device_id_type=MESH,
            ).start()
            return carry

        lax.fori_loop(0, devices - 1, send_rows, 0)
        pltpu.make_async_copy(
            dsend.at[m, pl.ds(pl.multiple_of((me // 2) * UNIT, UNIT), UNIT)],
            drecv.at[m, pl.ds(pl.multiple_of(me * UNIT, UNIT), UNIT)],
            dr_sem.at[m],
        ).start()

        @pl.when(jnp.logical_not(last_sec))
        def _():
            x_copy(m).start()

        @pl.when(jnp.logical_not(first_sec))
        def _():
            hid_copy(m).start()

        @pl.when(m == 0)
        def _():
            permutations()
            for copy in weight_copies:
                copy.wait()

        wait_block(drecv.at[m], dr_sem.at[m])
        span = GROUP * CAP
        for g in range(groups):
            rows = drecv[m, g * GROUP * UNIT : (g + 1) * GROUP * UNIT]
            moved = matmul(perm_vm[...], rows).astype(BF16)
            for k in range(PIECES):
                arranged[g * span : (g + 1) * span, k * part_w : (k + 1) * part_w] = moved[
                    k * span : (k + 1) * span
                ]
        hidden_w = gate_vm.shape[1]
        block_n = min(256, hidden_w)
        lhs = arranged[...]
        for n in range(hidden_w // block_n):
            cols = slice(n * block_n, (n + 1) * block_n)
            gate = matmul(lhs, gate_vm[:, cols])
            up = matmul(lhs, up_vm[:, cols])
            act_vm[:, cols] = (gate / (1.0 + jnp.exp(-gate)) * up).astype(BF16)
        act = act_vm[...]
        for k in range(PIECES):
            part = matmul(act, down_vm[:, k * part_w : (k + 1) * part_w]).astype(BF16)
            for g in range(groups):
                part_vm[g, k * span : (k + 1) * span] = part[g * span : (g + 1) * span]
        for g in range(groups):
            rsend[m, g * GROUP * UNIT : (g + 1) * GROUP * UNIT] = matmul(
                permt_vm[...], part_vm[g]
            ).astype(BF16)

        def send_parts(i, carry):
            to = target(i)
            pltpu.make_async_remote_copy(
                src_ref=rsend.at[m, pl.ds(pl.multiple_of(to * UNIT, UNIT), UNIT)],
                dst_ref=rrecv.at[m + ret_base, pl.ds(pl.multiple_of(me * UNIT, UNIT), UNIT)],
                send_sem=rs_sem.at[m],
                recv_sem=rr_sem.at[m + ret_base],
                device_id=(nxt, to),
                device_id_type=MESH,
            ).start()
            return carry

        lax.fori_loop(0, devices - 1, send_parts, 0)

        own = pl.ds(pl.multiple_of(me * UNIT, UNIT), UNIT)

        @pl.when(last_sec)
        def _():
            pltpu.make_async_copy(
                rsend.at[m, own], rrecv.at[m + micro, own], rr_sem.at[m + micro]
            ).start()

        @pl.when(jnp.logical_not(last_sec))
        def _():
            pltpu.make_async_remote_copy(
                src_ref=rsend.at[m, own],
                dst_ref=rrecv.at[m, own],
                send_sem=rs_sem.at[m],
                recv_sem=rr_sem.at[m],
                device_id=(nxt, me),
                device_id_type=MESH,
            ).start()

        return carry

    pl.semaphore_wait(
        barrier,
        devices - 1 + jnp.where(last_sec, 0, devices) + jnp.where(first_sec, 0, 1),
    )

    @pl.when(jnp.logical_not(last_sec))
    def _():
        mix_copy.start()

    lax.fori_loop(0, micro, micro_batch, 0)

    @pl.when(last_sec)
    def _():
        def finish(m, carry):
            spread(mix_vm[m], m)
            wait_block(rrecv.at[m + micro], rr_sem.at[m + micro])
            done = combine(m, m + micro, pieces_of(x_vm[m]))
            for k in range(PIECES):
                out_ref[0, m, :, k * part_w : (k + 1) * part_w] = done[k]
            return carry

        lax.fori_loop(0, micro, finish, 0)

    @pl.when(jnp.logical_not(last_sec))
    def _():
        mix_copy.wait_send()

        def receive(m, carry):
            wait_block(hid_vm.at[m], hr_sem.at[m])
            out_ref[0, m] = hid_vm[m]
            x_copy(m).wait_send()
            return carry

        lax.fori_loop(0, micro, receive, 0)

    def drain(m, carry):
        others = pl.ds(0, (devices - 1) * UNIT)
        wait_block(rrecv.at[0, others], ds_sem.at[m])
        wait_block(rrecv.at[0, others], rs_sem.at[m])

        @pl.when(jnp.logical_not(last_sec))
        def _():
            wait_block(rrecv.at[0, pl.ds(0, UNIT)], rs_sem.at[m])

        @pl.when(jnp.logical_not(first_sec))
        def _():
            hid_copy(m).wait_send()

        return carry

    lax.fori_loop(0, micro, drain, 0)


def solution(mesh):
    sections, devices = mesh.shape["section"], mesh.shape["expert"]
    z_size = min(Z_SIZE, devices // 2)

    def on_device(tokens, norm_gain, w_gate, w_up, w_down, routes, route_weights):
        micro, tok, width = tokens.shape
        hidden_w = w_gate.shape[2]
        part_w = width // PIECES
        vmem = pl.BlockSpec(memory_space=pltpu.VMEM)
        hbm = pl.BlockSpec(memory_space=pl.ANY)
        block = (devices * UNIT, part_w)
        span = GROUP * UNIT
        dma = pltpu.SemaphoreType.DMA
        return pl.pallas_call(
            functools.partial(kernel, sections, devices, z_size),
            out_shape=jax.ShapeDtypeStruct((1, micro, tok, width), BF16),
            in_specs=[vmem, vmem, hbm, hbm, hbm, vmem, vmem],
            out_specs=vmem,
            scratch_shapes=[
                pltpu.VMEM((width, hidden_w), BF16),
                pltpu.VMEM((width, hidden_w), BF16),
                pltpu.VMEM((hidden_w, width), BF16),
                pltpu.VMEM((micro, tok, width), BF16),
                pltpu.VMEM((micro, tok, width), BF16),
                pltpu.VMEM((micro, tok, width), BF16),
                pltpu.VMEM((micro, devices // 2 * UNIT, PIECES * tok), BF16),
                pltpu.VMEM((micro, 3 * PIECES * tok, devices * UNIT), BF16),
                pltpu.VMEM((micro, tok, devices * CAP), F32),
                pltpu.VMEM((micro, tok, devices * CAP), F32),
                pltpu.VMEM((span, span), BF16),
                pltpu.VMEM((span, span), BF16),
                pltpu.VMEM((micro, devices // 2 * UNIT, part_w), BF16),
                pltpu.VMEM((micro,) + block, BF16),
                pltpu.VMEM((micro,) + block, BF16),
                pltpu.VMEM((2 * micro,) + block, BF16),
                pltpu.VMEM((devices * CAP, width), BF16),
                pltpu.VMEM((devices * CAP, hidden_w), BF16),
                pltpu.VMEM((devices // GROUP, span, part_w), BF16),
                dma((3,)),
                dma((micro,)),
                dma((micro,)),
                dma((micro,)),
                dma((2 * micro,)),
                dma((micro,)),
                dma((micro,)),
                dma((micro,)),
                dma((micro,)),
                dma,
                dma,
            ],
            compiler_params=pltpu.CompilerParams(
                collective_id=0, has_side_effects=True, vmem_limit_bytes=56 << 20
            ),
        )(tokens, norm_gain, w_gate, w_up, w_down, routes, route_weights)

    in_specs = (
        P(None, "expert", None),
        P("section", None),
        P("section", None, "expert"),
        P("section", None, "expert"),
        P("section", "expert", None),
        P("section", None, "expert", None),
        P("section", None, "expert", None),
    )
    return jax.shard_map(
        on_device,
        mesh=mesh,
        in_specs=in_specs,
        out_specs=P("section", None, "expert", None),
        check_vma=False,
    )
```

```python
import functools

import jax
import jax.numpy as jnp
from jax import lax
from jax.experimental import pallas as pl
from jax.experimental.pallas import tpu as pltpu
from jax.sharding import PartitionSpec as P

MESH = pl.DeviceIdType.MESH
CAP = 4
PIECES = 4
UNIT = CAP * PIECES
GROUP = 16
Z_SIZE = 8

F32 = jnp.float32
BF16 = jnp.bfloat16
I32 = jnp.int32


def iota(shape, dim):
    return lax.broadcasted_iota(I32, shape, dim)


def matmul(a, b):
    return jnp.dot(a, b, preferred_element_type=F32)


def matmul_nt(a, b):
    return lax.dot_general(a, b, (((1,), (1,)), ((), ())), preferred_element_type=F32)


def far_first(step, size):
    half = (step + 1) // 2
    return size // 2 + half * (1 - 2 * (step % 2))


def kernel(
    sections,
    devices,
    z_size,
    tokens_ref,
    gain_ref,
    gate_hbm,
    up_hbm,
    down_hbm,
    routes_ref,
    weights_ref,
    out_ref,
    gate_vm,
    up_vm,
    down_vm,
    x_vm,
    prev_vm,
    hid_vm,
    pack_vm,
    pack_in,
    gain_in,
    zmat_vm,
    mix_vm,
    mix_in,
    perm_vm,
    permt_vm,
    dsend,
    drecv,
    rsend,
    rrecv,
    arranged,
    act_vm,
    part_vm,
    w_sem,
    ds_sem,
    dr_sem,
    rs_sem,
    rr_sem,
    xs_sem,
    xr_sem,
    hs_sem,
    hr_sem,
    ms_sem,
    mr_sem,
    ps_sem,
    pr_sem,
):
    sec = lax.axis_index("section")
    me = lax.axis_index("expert")
    micro, tok, width = x_vm.shape
    part_w = width // PIECES
    experts = devices // 2
    slots = experts * CAP
    y_size = devices // z_size
    groups = devices // GROUP
    last = sections - 1
    first_sec = sec == 0
    last_sec = sec == last

    def home1(layer):
        return lax.rem(layer + sections - 2 + 4 * lax.rem(layer, 2), sections)

    hosted = lax.rem(sec + sections + 2 - 4 * lax.rem(sec, 2), sections)
    nxt = jnp.minimum(sec + 1, last)
    prv = jnp.maximum(sec - 1, 0)
    nxt1 = jnp.where(last_sec, last, home1(nxt))
    ret_base = jnp.where(last_sec, micro, 0)

    weight_copies = [
        pltpu.make_async_copy(gate_hbm.at[0], gate_vm, w_sem.at[0]),
        pltpu.make_async_copy(up_hbm.at[0], up_vm, w_sem.at[1]),
        pltpu.make_async_copy(down_hbm.at[0], down_vm, w_sem.at[2]),
    ]
    for copy in weight_copies:
        copy.start()

    barrier = pltpu.get_barrier_semaphore()

    def greet(section, device):
        pl.semaphore_signal(barrier, inc=1, device_id=(section, device), device_id_type=MESH)

    def greet_all(section, start):
        def step(i, carry):
            greet(section, lax.rem(me + i, devices))
            return carry

        lax.fori_loop(start, devices, step, 0)

    greet_all(sec, 1)
    greet_all(home1(sec), 0)
    greet(hosted, me)

    @pl.when(jnp.logical_not(first_sec))
    def _():
        greet_all(prv, 0)

    @pl.when(hosted > 0)
    def _():
        greet_all(hosted - 1, 0)
        greet(home1(hosted - 1), me)

    @pl.when(jnp.logical_not(last_sec))
    def _():
        greet(nxt, me)
        greet(nxt1, me)

    @pl.when(last_sec)
    def _():
        greet(home1(last), me)

    def tables(m, carry):
        picked = routes_ref[0, m]
        share = weights_ref[0, m]
        choice = jnp.concatenate([picked[:, 0:1], picked[:, 1:2]], axis=0)
        scale = jnp.concatenate([share[:, 0:1], share[:, 1:2]], axis=0)
        count = 2 * tok
        onehot = (choice == iota((count, experts), 1)).astype(F32)
        below = (iota((count, count), 1) < iota((count, count), 0)).astype(BF16)
        earlier = matmul(below, onehot.astype(BF16))
        slot = jnp.sum(earlier * onehot, axis=1, keepdims=True).astype(I32)
        place = choice * CAP + slot
        hit = (place == iota((count, slots), 1)).astype(F32)
        index_row = iota((8, slots), 1).astype(BF16)
        row0 = matmul_nt(index_row, jnp.concatenate([hit[:tok]] * PIECES, axis=0).astype(BF16))
        row1 = matmul_nt(index_row, jnp.concatenate([hit[tok:]] * PIECES, axis=0).astype(BF16))
        shape = (experts * UNIT, PIECES * tok)
        r, c = iota(shape, 0), iota(shape, 1)
        want = (r // UNIT) * CAP + r % CAP
        same = (r // CAP) % PIECES == c // tok
        names = (row0[0:1].astype(I32) == want) | (row1[0:1].astype(I32) == want)
        pack_vm[m] = (names & same).astype(F32).astype(BF16)
        lane = iota((count, devices * CAP), 1)
        lands = (lane // (2 * CAP)) * CAP + lane % CAP == place
        weighted = jnp.where(lands, scale, 0.0)
        mix_vm[m] = weighted[:tok] + weighted[tok:]
        return carry

    def spread(mix, m):
        high = mix.astype(BF16)
        rest = mix - high.astype(F32)
        mid = rest.astype(BF16)
        low = (rest - mid.astype(F32)).astype(BF16)
        terms = jnp.concatenate([high, mid, low], axis=0)
        shape = (devices * CAP, devices * UNIT)
        j, c = iota(shape, 0), iota(shape, 1)
        widen = ((c // UNIT == j // CAP) & (c % CAP == j % CAP)).astype(F32).astype(BF16)
        wide = matmul(terms, widen)
        lane = iota((tok, devices * UNIT), 1)
        rows = []
        for term in range(3):
            block = wide[term * tok : (term + 1) * tok]
            for piece in range(PIECES):
                rows.append(jnp.where((lane // CAP) % PIECES == piece, block, 0.0))
        zmat_vm[m] = jnp.concatenate(rows, axis=0).astype(BF16)

    def permutations():
        size = GROUP * UNIT
        r, c = iota((size, size), 0), iota((size, size), 1)

        def moved(a, b):
            return (
                (a // (GROUP * CAP) == (b // CAP) % PIECES)
                & ((a // CAP) % GROUP == b // UNIT)
                & (a % CAP == b % CAP)
            )

        perm_vm[...] = moved(r, c).astype(F32).astype(BF16)
        permt_vm[...] = moved(c, r).astype(F32).astype(BF16)

    lax.fori_loop(0, micro, tables, 0)

    def send(src, dst, send_sem, recv_sem, section, device):
        return pltpu.make_async_remote_copy(
            src_ref=src,
            dst_ref=dst,
            send_sem=send_sem,
            recv_sem=recv_sem,
            device_id=(section, device),
            device_id_type=MESH,
        )

    pl.semaphore_wait(
        barrier,
        2 * devices
        + 1
        + jnp.where(last_sec, 0, 2 * devices)
        + jnp.where(first_sec, 0, 1)
        + jnp.where(hosted == 0, 0, 1),
    )

    x_to = [nxt, jnp.where(hosted == last, last, home1(jnp.minimum(hosted + 1, last)))]
    x_slot = [0, jnp.where(hosted == last, micro, 1)]
    hid_to = [prv, jnp.maximum(hosted - 1, 0)]
    layer_of = [sec, hosted]

    def x_copy(m):
        return send(
            x_vm.at[m], prev_vm.at[x_slot[m]], xs_sem.at[m], xr_sem.at[x_slot[m]], x_to[m], me
        )

    def hid_copy(m):
        return send(x_vm.at[m], hid_vm.at[m], hs_sem.at[m], hr_sem.at[m], hid_to[m], me)

    def mix_copy(m, to):
        return send(mix_vm.at[m], mix_in.at[m], ms_sem.at[m], mr_sem.at[m], to, me)

    def pack_copy():
        return send(pack_vm.at[1], pack_in, ps_sem.at[0], pr_sem.at[0], home1(sec), me)

    def gain_copy():
        return send(gain_ref, gain_in, ps_sem.at[1], pr_sem.at[1], home1(sec), me)

    def wait_block(buffer, sem):
        pltpu.make_async_copy(buffer, buffer, sem).wait()

    def hand_out_tables():
        pack_copy().start()
        gain_copy().start()

        @pl.when(jnp.logical_not(last_sec))
        def _():
            mix_copy(0, nxt).start()
            mix_copy(1, nxt1).start()

    def pieces_of(value):
        return [value[:, k * part_w : (k + 1) * part_w] for k in range(PIECES)]

    def combine(z, base, x_pieces):
        total = matmul(zmat_vm[z], rrecv[base])
        rows = PIECES * tok
        summed = (total[2 * rows :] + total[rows : 2 * rows]) + total[:rows]
        return [
            (x_pieces[k].astype(F32) + summed[k * tok : (k + 1) * tok]).astype(BF16)
            for k in range(PIECES)
        ]

    def target(i):
        y = lax.rem(me // z_size + far_first(i % y_size, y_size), y_size)
        z = lax.rem(me % z_size + far_first(i // y_size, z_size), z_size)
        return y * z_size + z

    def block(index):
        return pl.ds(pl.multiple_of(index * UNIT, UNIT), UNIT)

    own = block(me)

    def home(m):
        layer = layer_of[m]

        @pl.when(layer == 0)
        def _():
            x_vm[m] = tokens_ref[m]

        @pl.when(layer > 0)
        def _():
            wait_block(mix_in.at[m], mr_sem.at[m])
            spread(mix_in[m], m)
            wait_block(prev_vm.at[m], xr_sem.at[m])
            wait_block(rrecv.at[m], rr_sem.at[m])
            done = combine(m, m, pieces_of(prev_vm[m]))
            for k in range(PIECES):
                x_vm[m, :, k * part_w : (k + 1) * part_w] = done[k]

        if m == 0:
            gain, pack = gain_ref[...], pack_vm[0]
        else:
            wait_block(pack_in, pr_sem.at[0])
            wait_block(gain_in, pr_sem.at[1])
            gain, pack = gain_in[...], pack_in[...]
        wide = x_vm[m].astype(F32)
        mean = jnp.mean(wide * wide, axis=-1, keepdims=True)
        normed = (wide * lax.rsqrt(mean + 1e-06) * gain).astype(BF16)
        stacked = jnp.concatenate(pieces_of(normed), axis=0)
        dsend[m] = matmul(pack, stacked).astype(BF16)

        def send_rows(i, carry):
            to = target(i)
            send(
                dsend.at[m, block(to // 2)],
                drecv.at[m, own],
                ds_sem.at[m],
                dr_sem.at[m],
                layer,
                to,
            ).start()
            return carry

        lax.fori_loop(0, devices - 1 + m, send_rows, 0)
        if m == 0:
            pltpu.make_async_copy(
                dsend.at[m, block(me // 2)], drecv.at[m, own], dr_sem.at[m]
            ).start()

        @pl.when(layer < last if m == 0 else layer >= 0)
        def _():
            x_copy(m).start()

        @pl.when(layer > 0)
        def _():
            hid_copy(m).start()

    def expert(m, carry):
        @pl.when(m == 0)
        def _():
            for copy in weight_copies:
                copy.wait()

        wait_block(drecv.at[m], dr_sem.at[m])
        span = GROUP * CAP
        for g in range(groups):
            rows = drecv[m, g * GROUP * UNIT : (g + 1) * GROUP * UNIT]
            moved = matmul(perm_vm[...], rows).astype(BF16)
            for k in range(PIECES):
                arranged[g * span : (g + 1) * span, k * part_w : (k + 1) * part_w] = moved[
                    k * span : (k + 1) * span
                ]
        hidden_w = gate_vm.shape[1]
        block_n = min(256, hidden_w)
        lhs = arranged[...]
        for n in range(hidden_w // block_n):
            cols = slice(n * block_n, (n + 1) * block_n)
            gate = matmul(lhs, gate_vm[:, cols])
            up = matmul(lhs, up_vm[:, cols])
            act_vm[:, cols] = (gate / (1.0 + jnp.exp(-gate)) * up).astype(BF16)
        act = act_vm[...]
        for k in range(PIECES):
            part = matmul(act, down_vm[:, k * part_w : (k + 1) * part_w]).astype(BF16)
            for g in range(groups):
                part_vm[g, k * span : (k + 1) * span] = part[g * span : (g + 1) * span]
        for g in range(groups):
            rsend[m, g * GROUP * UNIT : (g + 1) * GROUP * UNIT] = matmul(
                permt_vm[...], part_vm[g]
            ).astype(BF16)

        section = jnp.where(m == 0, nxt, nxt1)
        slot = m + ret_base

        def send_parts(i, carry):
            to = target(i)
            send(
                rsend.at[m, block(to)],
                rrecv.at[slot, own],
                rs_sem.at[m],
                rr_sem.at[slot],
                section,
                to,
            ).start()
            return carry

        lax.fori_loop(0, devices - jnp.where(last_sec, 1, 0), send_parts, 0)

        @pl.when(last_sec)
        def _():
            pltpu.make_async_copy(rsend.at[m, own], rrecv.at[slot, own], rr_sem.at[slot]).start()

        return carry

    early = ((lax.rem(sec, 2) == 1) & (hosted < last)) | (hosted == 0)

    @pl.when(first_sec)
    def _():
        home(0)
        hand_out_tables()
        permutations()

    @pl.when(jnp.logical_not(first_sec))
    def _():
        hand_out_tables()
        permutations()

    @pl.when(early)
    def _():
        home(1)

    @pl.when(jnp.logical_not(first_sec))
    def _():
        home(0)

    lax.fori_loop(0, micro, expert, 0)

    @pl.when(jnp.logical_not(early))
    def _():
        home(1)

    @pl.when(last_sec)
    def _():
        wait_block(prev_vm.at[micro], xr_sem.at[micro])
        for m in range(micro):
            spread(mix_vm[m], m)
            wait_block(rrecv.at[m + micro], rr_sem.at[m + micro])
            x_ref = x_vm.at[0] if m == 0 else prev_vm.at[micro]
            done = combine(m, m + micro, pieces_of(x_ref[...]))
            for k in range(PIECES):
                out_ref[0, m, :, k * part_w : (k + 1) * part_w] = done[k]

    @pl.when(jnp.logical_not(last_sec))
    def _():
        mix_copy(0, nxt).wait_send()
        mix_copy(1, nxt1).wait_send()
        x_copy(0).wait_send()
        for m in range(micro):
            wait_block(hid_vm.at[m], hr_sem.at[m])
            out_ref[0, m] = hid_vm[m]

    pack_copy().wait_send()
    gain_copy().wait_send()
    x_copy(1).wait_send()
    most = pl.ds(0, (devices - 1) * UNIT)
    one = pl.ds(0, UNIT)
    for m in range(micro):
        wait_block(rrecv.at[0, most], ds_sem.at[m])
        wait_block(rrecv.at[0, most], rs_sem.at[m])

        @pl.when(jnp.logical_not(last_sec))
        def _():
            wait_block(rrecv.at[0, one], rs_sem.at[m])

        @pl.when(layer_of[m] > 0)
        def _():
            hid_copy(m).wait_send()

    wait_block(rrecv.at[0, one], ds_sem.at[1])


def solution(mesh):
    sections, devices = mesh.shape["section"], mesh.shape["expert"]
    z_size = min(Z_SIZE, devices // 2)

    def on_device(tokens, norm_gain, w_gate, w_up, w_down, routes, route_weights):
        micro, tok, width = tokens.shape
        hidden_w = w_gate.shape[2]
        part_w = width // PIECES
        vmem = pl.BlockSpec(memory_space=pltpu.VMEM)
        hbm = pl.BlockSpec(memory_space=pl.ANY)
        block = (devices * UNIT, part_w)
        span = GROUP * UNIT
        dma = pltpu.SemaphoreType.DMA
        return pl.pallas_call(
            functools.partial(kernel, sections, devices, z_size),
            out_shape=jax.ShapeDtypeStruct((1, micro, tok, width), BF16),
            in_specs=[vmem, vmem, hbm, hbm, hbm, vmem, vmem],
            out_specs=vmem,
            scratch_shapes=[
                pltpu.VMEM((width, hidden_w), BF16),
                pltpu.VMEM((width, hidden_w), BF16),
                pltpu.VMEM((hidden_w, width), BF16),
                pltpu.VMEM((micro, tok, width), BF16),
                pltpu.VMEM((micro + 1, tok, width), BF16),
                pltpu.VMEM((micro, tok, width), BF16),
                pltpu.VMEM((micro, devices // 2 * UNIT, PIECES * tok), BF16),
                pltpu.VMEM((devices // 2 * UNIT, PIECES * tok), BF16),
                pltpu.VMEM((1, width), F32),
                pltpu.VMEM((micro, 3 * PIECES * tok, devices * UNIT), BF16),
                pltpu.VMEM((micro, tok, devices * CAP), F32),
                pltpu.VMEM((micro, tok, devices * CAP), F32),
                pltpu.VMEM((span, span), BF16),
                pltpu.VMEM((span, span), BF16),
                pltpu.VMEM((micro, devices // 2 * UNIT, part_w), BF16),
                pltpu.VMEM((micro,) + block, BF16),
                pltpu.VMEM((micro,) + block, BF16),
                pltpu.VMEM((2 * micro,) + block, BF16),
                pltpu.VMEM((devices * CAP, width), BF16),
                pltpu.VMEM((devices * CAP, hidden_w), BF16),
                pltpu.VMEM((devices // GROUP, span, part_w), BF16),
                dma((3,)),
                dma((micro,)),
                dma((micro,)),
                dma((micro,)),
                dma((2 * micro,)),
                dma((micro,)),
                dma((micro + 1,)),
                dma((micro,)),
                dma((micro,)),
                dma((micro,)),
                dma((micro,)),
                dma((2,)),
                dma((2,)),
            ],
            compiler_params=pltpu.CompilerParams(
                collective_id=0, has_side_effects=True, vmem_limit_bytes=56 << 20
            ),
        )(tokens, norm_gain, w_gate, w_up, w_down, routes, route_weights)

    in_specs = (
        P(None, "expert", None),
        P("section", None),
        P("section", None, "expert"),
        P("section", None, "expert"),
        P("section", "expert", None),
        P("section", None, "expert", None),
        P("section", None, "expert", None),
    )
    return jax.shard_map(
        on_device,
        mesh=mesh,
        in_specs=in_specs,
        out_specs=P("section", None, "expert", None),
        check_vma=False,
    )
```

```python
import functools

import jax
import jax.numpy as jnp
from jax import lax
from jax.experimental import pallas as pl
from jax.experimental.pallas import tpu as pltpu
from jax.sharding import PartitionSpec as P

MESH = pl.DeviceIdType.MESH
CAP = 4
PIECES = 4
UNIT = CAP * PIECES
GROUP = 16
Z_SIZE = 8

F32 = jnp.float32
BF16 = jnp.bfloat16
I32 = jnp.int32


def iota(shape, dim):
    return lax.broadcasted_iota(I32, shape, dim)


def matmul(a, b):
    return jnp.dot(a, b, preferred_element_type=F32)


def matmul_nt(a, b):
    return lax.dot_general(a, b, (((1,), (1,)), ((), ())), preferred_element_type=F32)


def far_first(step, size):
    half = (step + 1) // 2
    return size // 2 + half * (1 - 2 * (step % 2))


def kernel(
    sections,
    devices,
    z_size,
    tokens_ref,
    gain_ref,
    gate_hbm,
    up_hbm,
    down_hbm,
    routes_ref,
    weights_ref,
    out_ref,
    gate_vm,
    up_vm,
    down_vm,
    x_vm,
    prev_vm,
    hid_vm,
    pack_vm,
    pack_in,
    gain_in,
    zmat_vm,
    mix_vm,
    mix_in,
    perm_vm,
    permt_vm,
    dsend,
    drecv,
    rsend,
    rrecv,
    arranged,
    act_vm,
    part_vm,
    w_sem,
    ds_sem,
    dr_sem,
    rs_sem,
    rr_sem,
    xs_sem,
    xr_sem,
    hs_sem,
    hr_sem,
    ms_sem,
    mr_sem,
    ps_sem,
    pr_sem,
):
    sec = lax.axis_index("section")
    me = lax.axis_index("expert")
    micro, tok, width = x_vm.shape
    part_w = width // PIECES
    experts = devices // 2
    slots = experts * CAP
    y_size = devices // z_size
    groups = devices // GROUP
    last = sections - 1
    first_sec = sec == 0
    last_sec = sec == last

    def home1(layer):
        return lax.rem(layer + sections - 2 + 4 * lax.rem(layer, 2), sections)

    hosted = lax.rem(sec + sections + 2 - 4 * lax.rem(sec, 2), sections)
    nxt = jnp.minimum(sec + 1, last)
    prv = jnp.maximum(sec - 1, 0)
    nxt1 = jnp.where(last_sec, last, home1(nxt))
    ret_base = jnp.where(last_sec, micro, 0)

    weight_copies = [
        pltpu.make_async_copy(gate_hbm.at[0], gate_vm, w_sem.at[0]),
        pltpu.make_async_copy(up_hbm.at[0], up_vm, w_sem.at[1]),
        pltpu.make_async_copy(down_hbm.at[0], down_vm, w_sem.at[2]),
    ]
    for copy in weight_copies:
        copy.start()

    barrier = pltpu.get_barrier_semaphore()

    def greet(section, device):
        pl.semaphore_signal(barrier, inc=1, device_id=(section, device), device_id_type=MESH)

    greet(hosted, me)

    @pl.when(first_sec)
    def _():
        def step(i, carry):
            greet(sec, lax.rem(me + i, devices))
            return carry

        lax.fori_loop(1, devices, step, 0)

    @pl.when(jnp.logical_not(first_sec))
    def _():
        greet(prv, me)

    @pl.when(hosted > 0)
    def _():
        greet(hosted - 1, me)
        greet(home1(hosted - 1), me)

    @pl.when(jnp.logical_not(last_sec))
    def _():
        greet(nxt, me)
        greet(nxt1, me)

    @pl.when(last_sec)
    def _():
        greet(home1(last), me)

    def tables(m, carry):
        picked = routes_ref[0, m]
        share = weights_ref[0, m]
        choice = jnp.concatenate([picked[:, 0:1], picked[:, 1:2]], axis=0)
        scale = jnp.concatenate([share[:, 0:1], share[:, 1:2]], axis=0)
        count = 2 * tok
        onehot = (choice == iota((count, experts), 1)).astype(F32)
        below = (iota((count, count), 1) < iota((count, count), 0)).astype(BF16)
        earlier = matmul(below, onehot.astype(BF16))
        slot = jnp.sum(earlier * onehot, axis=1, keepdims=True).astype(I32)
        place = choice * CAP + slot
        hit = (place == iota((count, slots), 1)).astype(F32)
        index_row = iota((8, slots), 1).astype(BF16)
        row0 = matmul_nt(index_row, jnp.concatenate([hit[:tok]] * PIECES, axis=0).astype(BF16))
        row1 = matmul_nt(index_row, jnp.concatenate([hit[tok:]] * PIECES, axis=0).astype(BF16))
        shape = (experts * UNIT, PIECES * tok)
        r, c = iota(shape, 0), iota(shape, 1)
        want = (r // UNIT) * CAP + r % CAP
        same = (r // CAP) % PIECES == c // tok
        names = (row0[0:1].astype(I32) == want) | (row1[0:1].astype(I32) == want)
        pack_vm[m] = (names & same).astype(F32).astype(BF16)
        lane = iota((count, devices * CAP), 1)
        lands = (lane // (2 * CAP)) * CAP + lane % CAP == place
        weighted = jnp.where(lands, scale, 0.0)
        mix_vm[m] = weighted[:tok] + weighted[tok:]
        return carry

    def spread(mix, m):
        high = mix.astype(BF16)
        rest = mix - high.astype(F32)
        mid = rest.astype(BF16)
        low = (rest - mid.astype(F32)).astype(BF16)
        terms = jnp.concatenate([high, mid, low], axis=0)
        shape = (devices * CAP, devices * UNIT)
        j, c = iota(shape, 0), iota(shape, 1)
        widen = ((c // UNIT == j // CAP) & (c % CAP == j % CAP)).astype(F32).astype(BF16)
        wide = matmul(terms, widen)
        lane = iota((tok, devices * UNIT), 1)
        rows = []
        for term in range(3):
            block = wide[term * tok : (term + 1) * tok]
            for piece in range(PIECES):
                rows.append(jnp.where((lane // CAP) % PIECES == piece, block, 0.0))
        zmat_vm[m] = jnp.concatenate(rows, axis=0).astype(BF16)

    def permutations():
        size = GROUP * UNIT
        r, c = iota((size, size), 0), iota((size, size), 1)

        def moved(a, b):
            return (
                (a // (GROUP * CAP) == (b // CAP) % PIECES)
                & ((a // CAP) % GROUP == b // UNIT)
                & (a % CAP == b % CAP)
            )

        perm_vm[...] = moved(r, c).astype(F32).astype(BF16)
        permt_vm[...] = moved(c, r).astype(F32).astype(BF16)

    lax.fori_loop(0, micro, tables, 0)

    def send(src, dst, send_sem, recv_sem, section, device):
        return pltpu.make_async_remote_copy(
            src_ref=src,
            dst_ref=dst,
            send_sem=send_sem,
            recv_sem=recv_sem,
            device_id=(section, device),
            device_id_type=MESH,
        )

    pl.semaphore_wait(
        barrier,
        4 + jnp.where(first_sec, devices - 2, 0) + jnp.where(last_sec, 0, 2),
    )

    @pl.when(first_sec)
    def _():
        greet(home1(sec), me)

    x_to = [nxt, jnp.where(hosted == last, last, home1(jnp.minimum(hosted + 1, last)))]
    x_slot = [0, jnp.where(hosted == last, micro, 1)]
    hid_to = [prv, jnp.maximum(hosted - 1, 0)]
    layer_of = [sec, hosted]

    def x_copy(m):
        return send(
            x_vm.at[m], prev_vm.at[x_slot[m]], xs_sem.at[m], xr_sem.at[x_slot[m]], x_to[m], me
        )

    def hid_copy(m):
        return send(x_vm.at[m], hid_vm.at[m], hs_sem.at[m], hr_sem.at[m], hid_to[m], me)

    def mix_copy(m, to):
        return send(mix_vm.at[m], mix_in.at[m], ms_sem.at[m], mr_sem.at[m], to, me)

    def pack_copy():
        return send(pack_vm.at[1], pack_in, ps_sem.at[0], pr_sem.at[0], home1(sec), me)

    def gain_copy():
        return send(gain_ref, gain_in, ps_sem.at[1], pr_sem.at[1], home1(sec), me)

    def wait_block(buffer, sem):
        pltpu.make_async_copy(buffer, buffer, sem).wait()

    def hand_out_tables():
        pack_copy().start()
        gain_copy().start()

        @pl.when(jnp.logical_not(last_sec))
        def _():
            mix_copy(0, nxt).start()
            mix_copy(1, nxt1).start()

    def pieces_of(value):
        return [value[:, k * part_w : (k + 1) * part_w] for k in range(PIECES)]

    def combine(z, base, x_pieces):
        total = matmul(zmat_vm[z], rrecv[base])
        rows = PIECES * tok
        summed = (total[2 * rows :] + total[rows : 2 * rows]) + total[:rows]
        return [
            (x_pieces[k].astype(F32) + summed[k * tok : (k + 1) * tok]).astype(BF16)
            for k in range(PIECES)
        ]

    def target(i):
        y = lax.rem(me // z_size + far_first(i % y_size, y_size), y_size)
        z = lax.rem(me % z_size + far_first(i // y_size, z_size), z_size)
        return y * z_size + z

    def block(index):
        return pl.ds(pl.multiple_of(index * UNIT, UNIT), UNIT)

    own = block(me)

    def home(m):
        layer = layer_of[m]

        @pl.when(layer == 0)
        def _():
            x_vm[m] = tokens_ref[m]

        @pl.when(layer > 0)
        def _():
            wait_block(mix_in.at[m], mr_sem.at[m])
            spread(mix_in[m], m)
            wait_block(prev_vm.at[m], xr_sem.at[m])
            wait_block(rrecv.at[m], rr_sem.at[m])
            done = combine(m, m, pieces_of(prev_vm[m]))
            for k in range(PIECES):
                x_vm[m, :, k * part_w : (k + 1) * part_w] = done[k]

        if m == 0:
            gain, pack = gain_ref[...], pack_vm[0]
        else:
            wait_block(pack_in, pr_sem.at[0])
            wait_block(gain_in, pr_sem.at[1])
            gain, pack = gain_in[...], pack_in[...]
        wide = x_vm[m].astype(F32)
        mean = jnp.mean(wide * wide, axis=-1, keepdims=True)
        normed = (wide * lax.rsqrt(mean + 1e-06) * gain).astype(BF16)
        stacked = jnp.concatenate(pieces_of(normed), axis=0)
        dsend[m] = matmul(pack, stacked).astype(BF16)

        def send_rows(i):
            to = target(i)
            send(
                dsend.at[m, block(to // 2)],
                drecv.at[m, own],
                ds_sem.at[m],
                dr_sem.at[m],
                layer,
                to,
            ).start()

        for i in range(devices - 1 + m):
            send_rows(i)
        if m == 0:
            pltpu.make_async_copy(
                dsend.at[m, block(me // 2)], drecv.at[m, own], dr_sem.at[m]
            ).start()

        @pl.when(layer < last if m == 0 else layer >= 0)
        def _():
            x_copy(m).start()

        @pl.when(layer > 0)
        def _():
            hid_copy(m).start()

    def expert(m, carry):
        @pl.when(m == 0)
        def _():
            for copy in weight_copies:
                copy.wait()

        wait_block(drecv.at[m], dr_sem.at[m])
        span = GROUP * CAP
        for g in range(groups):
            rows = drecv[m, g * GROUP * UNIT : (g + 1) * GROUP * UNIT]
            moved = matmul(perm_vm[...], rows).astype(BF16)
            for k in range(PIECES):
                arranged[g * span : (g + 1) * span, k * part_w : (k + 1) * part_w] = moved[
                    k * span : (k + 1) * span
                ]
        hidden_w = gate_vm.shape[1]
        block_n = min(256, hidden_w)
        lhs = arranged[...]
        for n in range(hidden_w // block_n):
            cols = slice(n * block_n, (n + 1) * block_n)
            gate = matmul(lhs, gate_vm[:, cols])
            up = matmul(lhs, up_vm[:, cols])
            act_vm[:, cols] = (gate / (1.0 + jnp.exp(-gate)) * up).astype(BF16)
        act = act_vm[...]
        for k in range(PIECES):
            part = matmul(act, down_vm[:, k * part_w : (k + 1) * part_w]).astype(BF16)
            for g in range(groups):
                part_vm[g, k * span : (k + 1) * span] = part[g * span : (g + 1) * span]
        for g in range(groups):
            rsend[m, g * GROUP * UNIT : (g + 1) * GROUP * UNIT] = matmul(
                permt_vm[...], part_vm[g]
            ).astype(BF16)

        section = jnp.where(m == 0, nxt, nxt1)
        slot = m + ret_base

        def send_parts(i):
            to = target(i)
            send(
                rsend.at[m, block(to)],
                rrecv.at[slot, own],
                rs_sem.at[m],
                rr_sem.at[slot],
                section,
                to,
            ).start()

        for i in range(devices - 1):
            send_parts(i)

        @pl.when(jnp.logical_not(last_sec))
        def _():
            send_parts(devices - 1)

        @pl.when(last_sec)
        def _():
            pltpu.make_async_copy(rsend.at[m, own], rrecv.at[slot, own], rr_sem.at[slot]).start()

        return carry

    early = ((lax.rem(sec, 2) == 1) & (hosted < last)) | (hosted == 0)

    @pl.when(first_sec)
    def _():
        home(0)
        hand_out_tables()
        permutations()

    @pl.when(jnp.logical_not(first_sec))
    def _():
        hand_out_tables()
        permutations()

    @pl.when(early)
    def _():
        home(1)

    @pl.when(jnp.logical_not(first_sec))
    def _():
        home(0)

    lax.fori_loop(0, micro, expert, 0)

    @pl.when(jnp.logical_not(early))
    def _():
        home(1)

    @pl.when(last_sec)
    def _():
        wait_block(prev_vm.at[micro], xr_sem.at[micro])
        for m in range(micro):
            spread(mix_vm[m], m)
            wait_block(rrecv.at[m + micro], rr_sem.at[m + micro])
            x_ref = x_vm.at[0] if m == 0 else prev_vm.at[micro]
            done = combine(m, m + micro, pieces_of(x_ref[...]))
            for k in range(PIECES):
                out_ref[0, m, :, k * part_w : (k + 1) * part_w] = done[k]

    @pl.when(jnp.logical_not(last_sec))
    def _():
        mix_copy(0, nxt).wait_send()
        mix_copy(1, nxt1).wait_send()
        x_copy(0).wait_send()
        for m in range(micro):
            wait_block(hid_vm.at[m], hr_sem.at[m])
            out_ref[0, m] = hid_vm[m]

    pack_copy().wait_send()
    gain_copy().wait_send()
    x_copy(1).wait_send()
    most = pl.ds(0, (devices - 1) * UNIT)
    one = pl.ds(0, UNIT)
    for m in range(micro):
        wait_block(rrecv.at[0, most], ds_sem.at[m])
        wait_block(rrecv.at[0, most], rs_sem.at[m])

        @pl.when(jnp.logical_not(last_sec))
        def _():
            wait_block(rrecv.at[0, one], rs_sem.at[m])

        @pl.when(layer_of[m] > 0)
        def _():
            hid_copy(m).wait_send()

    wait_block(rrecv.at[0, one], ds_sem.at[1])


def solution(mesh):
    sections, devices = mesh.shape["section"], mesh.shape["expert"]
    z_size = min(Z_SIZE, devices // 2)

    def on_device(tokens, norm_gain, w_gate, w_up, w_down, routes, route_weights):
        micro, tok, width = tokens.shape
        hidden_w = w_gate.shape[2]
        part_w = width // PIECES
        vmem = pl.BlockSpec(memory_space=pltpu.VMEM)
        hbm = pl.BlockSpec(memory_space=pl.ANY)
        block = (devices * UNIT, part_w)
        span = GROUP * UNIT
        dma = pltpu.SemaphoreType.DMA
        return pl.pallas_call(
            functools.partial(kernel, sections, devices, z_size),
            out_shape=jax.ShapeDtypeStruct((1, micro, tok, width), BF16),
            in_specs=[vmem, vmem, hbm, hbm, hbm, vmem, vmem],
            out_specs=vmem,
            scratch_shapes=[
                pltpu.VMEM((width, hidden_w), BF16),
                pltpu.VMEM((width, hidden_w), BF16),
                pltpu.VMEM((hidden_w, width), BF16),
                pltpu.VMEM((micro, tok, width), BF16),
                pltpu.VMEM((micro + 1, tok, width), BF16),
                pltpu.VMEM((micro, tok, width), BF16),
                pltpu.VMEM((micro, devices // 2 * UNIT, PIECES * tok), BF16),
                pltpu.VMEM((devices // 2 * UNIT, PIECES * tok), BF16),
                pltpu.VMEM((1, width), F32),
                pltpu.VMEM((micro, 3 * PIECES * tok, devices * UNIT), BF16),
                pltpu.VMEM((micro, tok, devices * CAP), F32),
                pltpu.VMEM((micro, tok, devices * CAP), F32),
                pltpu.VMEM((span, span), BF16),
                pltpu.VMEM((span, span), BF16),
                pltpu.VMEM((micro, devices // 2 * UNIT, part_w), BF16),
                pltpu.VMEM((micro,) + block, BF16),
                pltpu.VMEM((micro,) + block, BF16),
                pltpu.VMEM((2 * micro,) + block, BF16),
                pltpu.VMEM((devices * CAP, width), BF16),
                pltpu.VMEM((devices * CAP, hidden_w), BF16),
                pltpu.VMEM((devices // GROUP, span, part_w), BF16),
                dma((3,)),
                dma((micro,)),
                dma((micro,)),
                dma((micro,)),
                dma((2 * micro,)),
                dma((micro,)),
                dma((micro + 1,)),
                dma((micro,)),
                dma((micro,)),
                dma((micro,)),
                dma((micro,)),
                dma((2,)),
                dma((2,)),
            ],
            compiler_params=pltpu.CompilerParams(
                collective_id=0, has_side_effects=True, vmem_limit_bytes=56 << 20
            ),
        )(tokens, norm_gain, w_gate, w_up, w_down, routes, route_weights)

    in_specs = (
        P(None, "expert", None),
        P("section", None),
        P("section", None, "expert"),
        P("section", None, "expert"),
        P("section", "expert", None),
        P("section", None, "expert", None),
        P("section", None, "expert", None),
    )
    return jax.shard_map(
        on_device,
        mesh=mesh,
        in_specs=in_specs,
        out_specs=P("section", None, "expert", None),
        check_vma=False,
    )
```

```python
import functools

import jax
import jax.numpy as jnp
from jax import lax
from jax.experimental import pallas as pl
from jax.experimental.pallas import tpu as pltpu
from jax.sharding import PartitionSpec as P

MESH = pl.DeviceIdType.MESH
CAP = 4
PIECES = 4
UNIT = CAP * PIECES
GROUP = 16
Z_SIZE = 8

F32 = jnp.float32
BF16 = jnp.bfloat16
I32 = jnp.int32


def iota(shape, dim):
    return lax.broadcasted_iota(I32, shape, dim)


def matmul(a, b):
    return jnp.dot(a, b, preferred_element_type=F32)


def matmul_nt(a, b):
    return lax.dot_general(a, b, (((1,), (1,)), ((), ())), preferred_element_type=F32)


def far_first(step, size):
    half = (step + 1) // 2
    return size // 2 + half * (1 - 2 * (step % 2))


def kernel(
    sections,
    devices,
    z_size,
    tokens_ref,
    gain_ref,
    gate_hbm,
    up_hbm,
    down_hbm,
    routes_ref,
    weights_ref,
    out_ref,
    gate_vm,
    up_vm,
    down_vm,
    x_vm,
    prev_vm,
    hid_vm,
    pack_vm,
    pack_in,
    gain_in,
    zmat_vm,
    mix_vm,
    mix_in,
    perm_vm,
    permt_vm,
    dsend,
    drecv,
    rsend,
    rrecv,
    arranged,
    act_vm,
    part_vm,
    w_sem,
    ds_sem,
    dr_sem,
    rs_sem,
    rr_sem,
    xs_sem,
    xr_sem,
    hs_sem,
    hr_sem,
    ms_sem,
    mr_sem,
    ps_sem,
    pr_sem,
):
    sec = lax.axis_index("section")
    me = lax.axis_index("expert")
    micro, tok, width = x_vm.shape
    part_w = width // PIECES
    experts = devices // 2
    slots = experts * CAP
    y_size = devices // z_size
    groups = devices // GROUP
    last = sections - 1
    first_sec = sec == 0
    last_sec = sec == last

    def home1(layer):
        return lax.rem(layer + sections - 2 + 4 * lax.rem(layer, 2), sections)

    hosted = lax.rem(sec + sections + 2 - 4 * lax.rem(sec, 2), sections)
    nxt = jnp.minimum(sec + 1, last)
    prv = jnp.maximum(sec - 1, 0)
    nxt1 = jnp.where(last_sec, last, home1(nxt))
    ret_base = jnp.where(last_sec, micro, 0)

    weight_copies = [
        pltpu.make_async_copy(gate_hbm.at[0], gate_vm, w_sem.at[0]),
        pltpu.make_async_copy(up_hbm.at[0], up_vm, w_sem.at[1]),
        pltpu.make_async_copy(down_hbm.at[0], down_vm, w_sem.at[2]),
    ]
    for copy in weight_copies:
        copy.start()

    barrier = pltpu.get_barrier_semaphore()

    def greet(section, device):
        pl.semaphore_signal(barrier, inc=1, device_id=(section, device), device_id_type=MESH)

    greet(hosted, me)

    @pl.when(first_sec)
    def _():
        def step(i, carry):
            greet(sec, lax.rem(me + i, devices))
            return carry

        lax.fori_loop(1, devices, step, 0)

    @pl.when(jnp.logical_not(first_sec))
    def _():
        greet(prv, me)

    @pl.when(hosted > 0)
    def _():
        greet(hosted - 1, me)
        greet(home1(hosted - 1), me)

    @pl.when(jnp.logical_not(last_sec))
    def _():
        greet(nxt, me)
        greet(nxt1, me)

    @pl.when(last_sec)
    def _():
        greet(home1(last), me)

    def tables(m, carry):
        picked = routes_ref[0, m]
        share = weights_ref[0, m]
        choice = jnp.concatenate([picked[:, 0:1], picked[:, 1:2]], axis=0)
        scale = jnp.concatenate([share[:, 0:1], share[:, 1:2]], axis=0)
        count = 2 * tok
        onehot = (choice == iota((count, experts), 1)).astype(F32)
        below = (iota((count, count), 1) < iota((count, count), 0)).astype(BF16)
        earlier = matmul(below, onehot.astype(BF16))
        slot = jnp.sum(earlier * onehot, axis=1, keepdims=True).astype(I32)
        place = choice * CAP + slot
        hit = (place == iota((count, slots), 1)).astype(F32)
        index_row = iota((8, slots), 1).astype(BF16)
        row0 = matmul_nt(index_row, jnp.concatenate([hit[:tok]] * PIECES, axis=0).astype(BF16))
        row1 = matmul_nt(index_row, jnp.concatenate([hit[tok:]] * PIECES, axis=0).astype(BF16))
        shape = (experts * UNIT, PIECES * tok)
        r, c = iota(shape, 0), iota(shape, 1)
        want = (r // UNIT) * CAP + r % CAP
        same = (r // CAP) % PIECES == c // tok
        names = (row0[0:1].astype(I32) == want) | (row1[0:1].astype(I32) == want)
        pack_vm[m] = (names & same).astype(F32).astype(BF16)
        lane = iota((count, devices * CAP), 1)
        lands = (lane // (2 * CAP)) * CAP + lane % CAP == place
        weighted = jnp.where(lands, scale, 0.0)
        mix_vm[m] = weighted[:tok] + weighted[tok:]
        return carry

    def spread(mix, m):
        high = mix.astype(BF16)
        rest = mix - high.astype(F32)
        mid = rest.astype(BF16)
        low = (rest - mid.astype(F32)).astype(BF16)
        terms = jnp.concatenate([high, mid, low], axis=0)
        shape = (devices * CAP, devices * UNIT)
        j, c = iota(shape, 0), iota(shape, 1)
        widen = ((c // UNIT == j // CAP) & (c % CAP == j % CAP)).astype(F32).astype(BF16)
        wide = matmul(terms, widen)
        lane = iota((tok, devices * UNIT), 1)
        rows = []
        for term in range(3):
            block = wide[term * tok : (term + 1) * tok]
            for piece in range(PIECES):
                rows.append(jnp.where((lane // CAP) % PIECES == piece, block, 0.0))
        zmat_vm[m] = jnp.concatenate(rows, axis=0).astype(BF16)

    def permutations():
        size = GROUP * UNIT
        r, c = iota((size, size), 0), iota((size, size), 1)

        def moved(a, b):
            return (
                (a // (GROUP * CAP) == (b // CAP) % PIECES)
                & ((a // CAP) % GROUP == b // UNIT)
                & (a % CAP == b % CAP)
            )

        perm_vm[...] = moved(r, c).astype(F32).astype(BF16)
        permt_vm[...] = moved(c, r).astype(F32).astype(BF16)

    lax.fori_loop(0, micro, tables, 0)

    def send(src, dst, send_sem, recv_sem, section, device):
        return pltpu.make_async_remote_copy(
            src_ref=src,
            dst_ref=dst,
            send_sem=send_sem,
            recv_sem=recv_sem,
            device_id=(section, device),
            device_id_type=MESH,
        )

    pl.semaphore_wait(
        barrier,
        4 + jnp.where(first_sec, devices - 2, 0) + jnp.where(last_sec, 0, 2),
    )

    @pl.when(first_sec)
    def _():
        greet(home1(sec), me)

    x_to = [nxt, jnp.where(hosted == last, last, home1(jnp.minimum(hosted + 1, last)))]
    x_slot = [0, jnp.where(hosted == last, micro, 1)]
    hid_to = [prv, jnp.maximum(hosted - 1, 0)]
    layer_of = [sec, hosted]

    def x_copy(m):
        return send(
            x_vm.at[m], prev_vm.at[x_slot[m]], xs_sem.at[m], xr_sem.at[x_slot[m]], x_to[m], me
        )

    def hid_copy(m):
        return send(x_vm.at[m], hid_vm.at[m], hs_sem.at[m], hr_sem.at[m], hid_to[m], me)

    def mix_copy(m, to):
        return send(mix_vm.at[m], mix_in.at[m], ms_sem.at[m], mr_sem.at[m], to, me)

    def pack_copy():
        return send(pack_vm.at[1], pack_in, ps_sem.at[0], pr_sem.at[0], home1(sec), me)

    def gain_copy():
        return send(gain_ref, gain_in, ps_sem.at[1], pr_sem.at[1], home1(sec), me)

    def wait_block(buffer, sem):
        pltpu.make_async_copy(buffer, buffer, sem).wait()

    def hand_out_tables():
        pack_copy().start()
        gain_copy().start()

        @pl.when(jnp.logical_not(last_sec))
        def _():
            mix_copy(0, nxt).start()
            mix_copy(1, nxt1).start()

    def pieces_of(value):
        return [value[:, k * part_w : (k + 1) * part_w] for k in range(PIECES)]

    def combine(z, base, x_pieces):
        total = matmul(zmat_vm[z], rrecv[base])
        rows = PIECES * tok
        summed = (total[2 * rows :] + total[rows : 2 * rows]) + total[:rows]
        return [
            (x_pieces[k].astype(F32) + summed[k * tok : (k + 1) * tok]).astype(BF16)
            for k in range(PIECES)
        ]

    def hops(step, size):
        return min(step, size - step)

    offsets = [(dy, dz) for dy in range(y_size) for dz in range(z_size)]
    offsets.sort(key=lambda o: (-hops(o[1], z_size) - hops(o[0], y_size), -hops(o[1], z_size), o[0], o[1]))

    def target(i):
        dy, dz = offsets[i]
        return lax.rem(me // z_size + dy, y_size) * z_size + lax.rem(me % z_size + dz, z_size)

    def block(index):
        return pl.ds(pl.multiple_of(index * UNIT, UNIT), UNIT)

    own = block(me)

    def home(m):
        layer = layer_of[m]

        @pl.when(layer == 0)
        def _():
            x_vm[m] = tokens_ref[m]

        @pl.when(layer > 0)
        def _():
            wait_block(mix_in.at[m], mr_sem.at[m])
            spread(mix_in[m], m)
            wait_block(prev_vm.at[m], xr_sem.at[m])
            wait_block(rrecv.at[m], rr_sem.at[m])
            done = combine(m, m, pieces_of(prev_vm[m]))
            for k in range(PIECES):
                x_vm[m, :, k * part_w : (k + 1) * part_w] = done[k]

        if m == 0:
            gain, pack = gain_ref[...], pack_vm[0]
        else:
            wait_block(pack_in, pr_sem.at[0])
            wait_block(gain_in, pr_sem.at[1])
            gain, pack = gain_in[...], pack_in[...]
        wide = x_vm[m].astype(F32)
        mean = jnp.mean(wide * wide, axis=-1, keepdims=True)
        normed = (wide * lax.rsqrt(mean + 1e-06) * gain).astype(BF16)
        stacked = jnp.concatenate(pieces_of(normed), axis=0)
        dsend[m] = matmul(pack, stacked).astype(BF16)

        def send_rows(i):
            to = target(i)
            send(
                dsend.at[m, block(to // 2)],
                drecv.at[m, own],
                ds_sem.at[m],
                dr_sem.at[m],
                layer,
                to,
            ).start()

        for i in range(devices - 1 + m):
            send_rows(i)
        if m == 0:
            pltpu.make_async_copy(
                dsend.at[m, block(me // 2)], drecv.at[m, own], dr_sem.at[m]
            ).start()

        @pl.when(layer < last if m == 0 else layer >= 0)
        def _():
            x_copy(m).start()

        @pl.when(layer > 0)
        def _():
            hid_copy(m).start()

    def expert(m, carry):
        @pl.when(m == 0)
        def _():
            for copy in weight_copies:
                copy.wait()

        wait_block(drecv.at[m], dr_sem.at[m])
        span = GROUP * CAP
        for g in range(groups):
            rows = drecv[m, g * GROUP * UNIT : (g + 1) * GROUP * UNIT]
            moved = matmul(perm_vm[...], rows).astype(BF16)
            for k in range(PIECES):
                arranged[g * span : (g + 1) * span, k * part_w : (k + 1) * part_w] = moved[
                    k * span : (k + 1) * span
                ]
        hidden_w = gate_vm.shape[1]
        block_n = min(256, hidden_w)
        lhs = arranged[...]
        for n in range(hidden_w // block_n):
            cols = slice(n * block_n, (n + 1) * block_n)
            gate = matmul(lhs, gate_vm[:, cols])
            up = matmul(lhs, up_vm[:, cols])
            act_vm[:, cols] = (gate / (1.0 + jnp.exp(-gate)) * up).astype(BF16)
        act = act_vm[...]
        for k in range(PIECES):
            part = matmul(act, down_vm[:, k * part_w : (k + 1) * part_w]).astype(BF16)
            for g in range(groups):
                part_vm[g, k * span : (k + 1) * span] = part[g * span : (g + 1) * span]
        for g in range(groups):
            rsend[m, g * GROUP * UNIT : (g + 1) * GROUP * UNIT] = matmul(
                permt_vm[...], part_vm[g]
            ).astype(BF16)

        section = jnp.where(m == 0, nxt, nxt1)
        slot = m + ret_base

        def send_parts(i):
            to = target(i)
            send(
                rsend.at[m, block(to)],
                rrecv.at[slot, own],
                rs_sem.at[m],
                rr_sem.at[slot],
                section,
                to,
            ).start()

        for i in range(devices - 1):
            send_parts(i)

        @pl.when(jnp.logical_not(last_sec))
        def _():
            send_parts(devices - 1)

        @pl.when(last_sec)
        def _():
            pltpu.make_async_copy(rsend.at[m, own], rrecv.at[slot, own], rr_sem.at[slot]).start()

        return carry

    early = ((lax.rem(sec, 2) == 1) & (hosted < last)) | (hosted == 0)

    @pl.when(first_sec)
    def _():
        home(0)
        hand_out_tables()
        permutations()

    @pl.when(jnp.logical_not(first_sec))
    def _():
        hand_out_tables()
        permutations()

    @pl.when(early)
    def _():
        home(1)

    @pl.when(jnp.logical_not(first_sec))
    def _():
        home(0)

    lax.fori_loop(0, micro, expert, 0)

    @pl.when(jnp.logical_not(early))
    def _():
        home(1)

    @pl.when(last_sec)
    def _():
        wait_block(prev_vm.at[micro], xr_sem.at[micro])
        for m in range(micro):
            spread(mix_vm[m], m)
            wait_block(rrecv.at[m + micro], rr_sem.at[m + micro])
            x_ref = x_vm.at[0] if m == 0 else prev_vm.at[micro]
            done = combine(m, m + micro, pieces_of(x_ref[...]))
            for k in range(PIECES):
                out_ref[0, m, :, k * part_w : (k + 1) * part_w] = done[k]

    @pl.when(jnp.logical_not(last_sec))
    def _():
        mix_copy(0, nxt).wait_send()
        mix_copy(1, nxt1).wait_send()
        x_copy(0).wait_send()
        for m in range(micro):
            wait_block(hid_vm.at[m], hr_sem.at[m])
            out_ref[0, m] = hid_vm[m]

    pack_copy().wait_send()
    gain_copy().wait_send()
    x_copy(1).wait_send()
    most = pl.ds(0, (devices - 1) * UNIT)
    one = pl.ds(0, UNIT)
    for m in range(micro):
        wait_block(rrecv.at[0, most], ds_sem.at[m])
        wait_block(rrecv.at[0, most], rs_sem.at[m])

        @pl.when(jnp.logical_not(last_sec))
        def _():
            wait_block(rrecv.at[0, one], rs_sem.at[m])

        @pl.when(layer_of[m] > 0)
        def _():
            hid_copy(m).wait_send()

    wait_block(rrecv.at[0, one], ds_sem.at[1])


def solution(mesh):
    sections, devices = mesh.shape["section"], mesh.shape["expert"]
    z_size = min(Z_SIZE, devices // 2)

    def on_device(tokens, norm_gain, w_gate, w_up, w_down, routes, route_weights):
        micro, tok, width = tokens.shape
        hidden_w = w_gate.shape[2]
        part_w = width // PIECES
        vmem = pl.BlockSpec(memory_space=pltpu.VMEM)
        hbm = pl.BlockSpec(memory_space=pl.ANY)
        block = (devices * UNIT, part_w)
        span = GROUP * UNIT
        dma = pltpu.SemaphoreType.DMA
        return pl.pallas_call(
            functools.partial(kernel, sections, devices, z_size),
            out_shape=jax.ShapeDtypeStruct((1, micro, tok, width), BF16),
            in_specs=[vmem, vmem, hbm, hbm, hbm, vmem, vmem],
            out_specs=vmem,
            scratch_shapes=[
                pltpu.VMEM((width, hidden_w), BF16),
                pltpu.VMEM((width, hidden_w), BF16),
                pltpu.VMEM((hidden_w, width), BF16),
                pltpu.VMEM((micro, tok, width), BF16),
                pltpu.VMEM((micro + 1, tok, width), BF16),
                pltpu.VMEM((micro, tok, width), BF16),
                pltpu.VMEM((micro, devices // 2 * UNIT, PIECES * tok), BF16),
                pltpu.VMEM((devices // 2 * UNIT, PIECES * tok), BF16),
                pltpu.VMEM((1, width), F32),
                pltpu.VMEM((micro, 3 * PIECES * tok, devices * UNIT), BF16),
                pltpu.VMEM((micro, tok, devices * CAP), F32),
                pltpu.VMEM((micro, tok, devices * CAP), F32),
                pltpu.VMEM((span, span), BF16),
                pltpu.VMEM((span, span), BF16),
                pltpu.VMEM((micro, devices // 2 * UNIT, part_w), BF16),
                pltpu.VMEM((micro,) + block, BF16),
                pltpu.VMEM((micro,) + block, BF16),
                pltpu.VMEM((2 * micro,) + block, BF16),
                pltpu.VMEM((devices * CAP, width), BF16),
                pltpu.VMEM((devices * CAP, hidden_w), BF16),
                pltpu.VMEM((devices // GROUP, span, part_w), BF16),
                dma((3,)),
                dma((micro,)),
                dma((micro,)),
                dma((micro,)),
                dma((2 * micro,)),
                dma((micro,)),
                dma((micro + 1,)),
                dma((micro,)),
                dma((micro,)),
                dma((micro,)),
                dma((micro,)),
                dma((2,)),
                dma((2,)),
            ],
            compiler_params=pltpu.CompilerParams(
                collective_id=0, has_side_effects=True, vmem_limit_bytes=56 << 20
            ),
        )(tokens, norm_gain, w_gate, w_up, w_down, routes, route_weights)

    in_specs = (
        P(None, "expert", None),
        P("section", None),
        P("section", None, "expert"),
        P("section", None, "expert"),
        P("section", "expert", None),
        P("section", None, "expert", None),
        P("section", None, "expert", None),
    )
    return jax.shard_map(
        on_device,
        mesh=mesh,
        in_specs=in_specs,
        out_specs=P("section", None, "expert", None),
        check_vma=False,
    )
```
